256 devices in a mesh: curve: 32 (over y_hi, z, core), tm: 8 (over y_lo, x).
Axes of the slice: x: 4, y: 4 (y_hi: 2, y_lo: 2; y = y_hi * 2 + y_lo), z: 8, core: 2. Of those that a mesh axis runs over, the one named last changes fastest.
Arguments:
- samples: float32 [8192, 65536], P('curve', 'tm'), may hold values from -30 to 30
- smoothing: float32 [8192], P('curve'), may hold values from 0.5 to 20
- test_matrix: float32 [4096, 64], P('tm'), may hold values from -0.75 to 0.75
- sketch_prev: float32 [4096, 64], P('tm', 'curve'), may hold values from -1.2 to 1.2
Outputs:
- coefficients: float32 [8192, 4096], P('curve', 'tm')
- scores: float32 [8192, 64], P('curve')
- sketch: float32 [4096, 64], P('tm', 'curve')
The draws below stay inside these ranges and needn't reach their ends.
All inputs are finite; a program needn't handle non-finite values.
Results may differ from the reference program's by a relative error of at most 0.0002.
Values sent between devices are 32-bit elements; how exact they have to be, the bound alone decides.
A program may use at most 64 MiB of HBM per device.

```python
import math
import jax
import jax.numpy as jnp
from jax import lax

K = 4096
SPB = 16
RANK = 64
ITERS = 4
CURVES = 8192
SAMPLES = 65536


def draw_samples(key, part):
    first_key, second_key = jax.random.split(jax.random.fold_in(key, 71))
    ramp = 1.0 + 2.0 * jnp.arange(CURVES, dtype=jnp.float32) / max(CURVES - 1, 1)
    noise = jax.random.truncated_normal(first_key, -6.0, 6.0, (CURVES, SAMPLES), jnp.float32)
    common = jax.random.truncated_normal(second_key, -6.0, 6.0, (SAMPLES,), jnp.float32)
    return jnp.clip(noise + ramp[:, None] * common[None, :], -30.0, 30.0)


def block_scale(own_key, dims, cuts, least, largest):
    level, own = 1.0, jax.random.fold_in(own_key, 6)
    for dim, shards_of in cuts:
        steps = jnp.exp(jax.random.uniform(jax.random.fold_in(own, dim), (shards_of,), jnp.float32, least / len(cuts), largest / len(cuts)))
        level = level * jnp.repeat(steps, dims[dim] // shards_of).reshape([-1 if axis == dim else 1 for axis in range(len(dims))])
    return level


def gaussian(rng, shape, deviation, reach, cuts=(), kind=jnp.bfloat16):
    values = jax.random.normal(rng, shape, jnp.float32) * deviation
    if len(cuts) > 0:
        values = block_scale(rng, shape, cuts, -0.22, 0.18) * values
    return jnp.clip(values, min=-reach, max=reach).astype(kind)


def setup_inputs(seed: int = 0) -> dict:
    splits = jax.random.split(jax.random.key(seed), 5)
    return {
        "samples": draw_samples(jax.random.fold_in(splits[4], 71), 0),
        "smoothing": jnp.clip(jnp.exp(math.log(20.0) - 3.6888795 * jax.random.uniform(splits[1], (CURVES,), jnp.float32) ** block_scale(splits[1], (CURVES,), ((0, 32),), -0.2, 0.2)), 0.5, 20.0),
        "test_matrix": gaussian(splits[2], (K, RANK), RANK ** -0.5, 0.75, ((0, 8),), jnp.float32),
        "sketch_prev": gaussian(splits[3], (K, RANK), 0.2, 1.2, ((0, 8), (1, 32)), jnp.float32),
    }


damping = 0.45


def weight_table():
    frac = (jnp.arange(SPB, dtype=jnp.float32) + 0.5) / SPB
    pieces = [frac ** 3 / 6.0, (-3.0 * frac ** 3 + 3.0 * frac ** 2 + 3.0 * frac + 1.0) / 6.0, (3.0 * frac ** 3 - 6.0 * frac ** 2 + 4.0) / 6.0, (1.0 - frac) ** 3 / 6.0]
    return jnp.stack(pieces) / SPB


def relax_sweep(widened, target, smooth_col, index_wide, total_basis):
    second = widened[:, 2:] - 2.0 * widened[:, 1:-1] + widened[:, :-2]
    in_range = (index_wide[:-2] >= 0) & (index_wide[:-2] <= total_basis - 3)
    second = jnp.where(in_range[None, :], second, 0.0)
    bending = second[:, 2:] - 2.0 * second[:, 1:-1] + second[:, :-2]
    interior = widened[:, 2:-2]
    column_index = index_wide[2:-2]
    penalty_diag = (column_index <= total_basis - 3).astype(jnp.float32) + 4.0 * ((column_index >= 1) & (column_index <= total_basis - 2)).astype(jnp.float32) + (column_index >= 2).astype(jnp.float32)
    return interior + damping * (target - interior - smooth_col * bending) / (1.0 + smooth_col * penalty_diag)


def reference(samples, smoothing, test_matrix, sketch_prev):
    row_count = samples.shape[0]
    blocks = samples.reshape(row_count, K, SPB)
    segment_sums = jnp.einsum("cgq,mq->mcg", blocks, weight_table(), precision=lax.Precision.HIGHEST)
    padded = jnp.pad(segment_sums, ((0, 0), (0, 0), (3, 3)))
    proj = padded[0, :, 0:K] + padded[1, :, 1:K + 1] + padded[2, :, 2:K + 2] + padded[3, :, 3:K + 3]
    smooth_col = smoothing[:, None]
    index_wide = jnp.arange(K + 4, dtype=jnp.int32) - 2
    coefficients = proj
    for sweep_number in range(ITERS):
        widened = jnp.pad(coefficients, ((0, 0), (2, 2)))
        coefficients = relax_sweep(widened, proj, smooth_col, index_wide, K)
    column_mean = jnp.sum(coefficients, axis=0) / CURVES
    centered = coefficients - column_mean[None, :]
    scores = jnp.dot(centered, test_matrix, precision=lax.Precision.HIGHEST, preferred_element_type=jnp.float32)
    sketch_part = jnp.einsum("ck,cr->kr", centered, scores, precision=lax.Precision.HIGHEST) / CURVES
    return coefficients, scores, sketch_prev + sketch_part
```

```python
import functools

import jax
import jax.numpy as jnp
import numpy as np
from jax import lax
from jax.experimental import pallas as pl
from jax.experimental.pallas import tpu as pltpu
from jax.sharding import PartitionSpec as P

SPB = 16
ITERS = 4
MARGIN = 2 * ITERS
LANES = 128
CHUNK = 1024
SEGS = CHUNK // SPB
SLOT = 16
GROUPS = LANES // SLOT
MESH = pl.DeviceIdType.MESH
damping = 0.45
TABLE_SCALE = 1.0 / (6.0 * 32.0**3 * SPB)


def banded_table():
    odd = 2 * np.arange(SPB, dtype=np.int64) + 1
    pieces = np.stack(
        [
            odd**3,
            -3 * odd**3 + 96 * odd**2 + 3072 * odd + 32768,
            3 * odd**3 - 192 * odd**2 + 4 * 32768,
            (32 - odd) ** 3,
        ]
    )
    band = np.zeros((CHUNK, LANES), np.float64)
    for segment in range(SEGS):
        for m in range(4):
            band[segment * SPB : (segment + 1) * SPB, segment + 3 - m] = pieces[m]
    high = band.astype(jnp.bfloat16)
    low = (band - high.astype(np.float64)).astype(jnp.bfloat16)
    return np.concatenate([high, low], axis=1)


def roll(value, shift):
    return pltpu.roll(value, shift % LANES, 1)


def kernel(
    curves,
    blocks,
    x_hbm,
    s_ref,
    tt_ref,
    prev_ref,
    w_hbm,
    coef_ref,
    score_ref,
    sketch_ref,
    xbuf,
    wbuf,
    obuf,
    smooth,
    to_left,
    to_right,
    from_left,
    from_right,
    local,
    msend,
    mall,
    lsend,
    lparts,
    lfull,
    usend,
    uparts,
    spack,
    sparts,
    x_sem,
    w_sem,
    halo_send,
    halo_recv,
    m_send,
    m_recv,
    rs_send,
    rs_recv,
    ag_send,
    ag_recv,
    u_send,
    u_recv,
    f_send,
    f_recv,
):
    rows, width = coef_ref.shape
    tiles = width // LANES
    chunks = x_hbm.shape[1] // CHUNK
    group = rows // GROUPS
    rank = tt_ref.shape[0]
    share = rank // blocks
    owned = rank // curves * tiles
    cg, tb = lax.axis_index("curve"), lax.axis_index("tm")
    left, right = lax.rem(tb + blocks - 1, blocks), lax.rem(tb + 1, blocks)

    def fetch(c):
        return pltpu.make_async_copy(x_hbm.at[:, pl.ds(c * CHUNK, CHUNK)], xbuf.at[c], x_sem.at[c])

    table_copy = pltpu.make_async_copy(w_hbm, wbuf, w_sem)
    fetch(0).start()
    table_copy.start()
    fetch(chunks - 1).start()
    for c in range(1, chunks - 1):
        fetch(c).start()

    barrier = pltpu.get_barrier_semaphore()

    @pl.loop(1, blocks)
    def _(k):
        pl.semaphore_signal(
            barrier, inc=1, device_id={"tm": lax.rem(tb + k, blocks)}, device_id_type=MESH
        )

    @pl.loop(1, curves)
    def _(k):
        pl.semaphore_signal(
            barrier, inc=1, device_id={"curve": lax.rem(cg + k, curves)}, device_id_type=MESH
        )

    line = s_ref.shape[1]
    for i in range(rows // line):
        smooth[pl.ds(i * line, line), :] = jnp.transpose(
            jnp.broadcast_to(s_ref[i : i + 1, :], (LANES, line))
        )

    def project(c):
        fetch(c).wait()
        x = xbuf[c]
        high = x.astype(jnp.bfloat16)
        rest = x - high.astype(jnp.float32)
        middle = rest.astype(jnp.bfloat16)
        low = (rest - middle.astype(jnp.float32)).astype(jnp.bfloat16)
        w = wbuf[...]
        total = jnp.dot(high, w, preferred_element_type=jnp.float32)
        total += jnp.dot(middle, w, preferred_element_type=jnp.float32)
        total += jnp.dot(low, w, preferred_element_type=jnp.float32)
        obuf[c] = (total[:, :LANES] + total[:, LANES:]) * TABLE_SCALE

    lane = lax.broadcasted_iota(jnp.int32, (group, LANES), 1)
    table_copy.wait()
    project(0)
    project(chunks - 1)
    packed_left = jnp.zeros((group, LANES), jnp.float32)
    packed_right = jnp.zeros((group, LANES), jnp.float32)
    last = SEGS - MARGIN
    for g in range(GROUPS):
        here = (lane >= g * SLOT) & (lane < (g + 1) * SLOT)
        at = pl.ds(g * group, group)
        packed_left = jnp.where(here, roll(obuf[0, at, :], g * SLOT), packed_left)
        packed_right = jnp.where(here, roll(obuf[chunks - 1, at, :], g * SLOT - last), packed_right)
    to_left[...] = packed_left
    to_right[...] = packed_right

    pl.semaphore_wait(barrier, blocks + curves - 2)

    def halo(side, source, target, device):
        return pltpu.make_async_remote_copy(
            src_ref=source,
            dst_ref=target,
            send_sem=halo_send.at[side],
            recv_sem=halo_recv.at[side],
            device_id={"tm": device},
            device_id_type=MESH,
        )

    send_left = halo(0, to_left, from_right, left)
    send_right = halo(1, to_right, from_left, right)
    send_left.start()
    send_right.start()

    @pl.loop(1, chunks - 1)
    def _(c):
        project(c)

    send_left.wait()
    send_right.wait()

    zero = jnp.zeros((), jnp.float32)
    has_left = jnp.where(tb > 0, 1.0, zero)
    has_right = jnp.where(tb < blocks - 1, 1.0, zero)
    first, final = tb == 0, tb == blocks - 1
    upper = lane >= LANES // 2

    def relax(g, sums):
        at = pl.ds(pl.multiple_of(g * group, group), group)
        arrived_left = pltpu.roll(from_left[...], lax.rem(LANES - MARGIN + LANES - g * SLOT, LANES), 1)
        arrived_right = pltpu.roll(from_right[...], lax.rem(LANES - g * SLOT, LANES), 1)
        arrived_left = arrived_left * has_left
        arrived_right = arrived_right * has_right
        spill = jnp.where(lane < 3, arrived_left, 0.0)
        target = []
        for i in range(tiles):
            odd = roll(obuf[2 * i + 1, at, :], LANES // 2)
            target.append(obuf[2 * i, at, :] + jnp.where(upper, odd, spill))
            spill = jnp.where(upper, 0.0, odd)
        outside = jnp.where(lane < MARGIN, arrived_right + spill, 0.0)
        target.append(jnp.where(lane >= LANES - MARGIN, arrived_left, outside))
        s = smooth[at, :]
        inner = damping / (1.0 + 6.0 * s)
        near = damping / (1.0 + 5.0 * s)
        edge = damping / (1.0 + s)
        step = [inner] * (tiles + 1)
        low_step = jnp.where(first & (lane == 0), edge, jnp.where(first & (lane == 1), near, step[0]))
        step[0] = low_step
        top = LANES - 1
        step[tiles - 1] = jnp.where(
            final & (lane == top), edge, jnp.where(final & (lane == top - 1), near, step[tiles - 1])
        )
        pull = [a * p for a, p in zip(step, target)]
        keep = [1.0 - a for a in step]
        bend = [a * s for a in step]
        count = tiles + 1

        def spread(values):
            up = [roll(v, -1) for v in values]
            down = [roll(v, 1) for v in values]
            out = []
            for i in range(count):
                nxt = jnp.where(lane == LANES - 1, up[(i + 1) % count], up[i])
                prv = jnp.where(lane == 0, down[(i - 1) % count], down[i])
                out.append(nxt + prv - 2.0 * values[i])
            return out

        c = target
        for _ in range(ITERS):
            second = spread(c)
            second[0] = jnp.where(first & (lane == 0), 0.0, second[0])
            second[tiles - 1] = jnp.where(final & (lane == LANES - 1), 0.0, second[tiles - 1])
            second[tiles] = jnp.where(
                (first & (lane == LANES - 1)) | (final & (lane == 0)), 0.0, second[tiles]
            )
            fourth = spread(second)
            c = [keep[i] * c[i] + pull[i] - bend[i] * fourth[i] for i in range(count)]
        out = []
        for i in range(tiles):
            coef_ref[at, pl.ds(i * LANES, LANES)] = c[i]
            out.append(sums[i] + c[i])
        return tuple(out)

    start = tuple(jnp.zeros((group, LANES), jnp.float32) for _ in range(tiles))
    sums = lax.fori_loop(0, GROUPS, relax, start)
    own_mean = [jnp.sum(v, axis=0, keepdims=True) / rows for v in sums]

    msend[...] = jnp.zeros_like(msend)
    for i in range(tiles):
        msend[i : i + 1, :] = own_mean[i]

    def mean_copy(k):
        return pltpu.make_async_remote_copy(
            src_ref=msend,
            dst_ref=mall.at[cg],
            send_sem=m_send.at[k],
            recv_sem=m_recv.at[k],
            device_id={"curve": lax.rem(cg + k, curves)},
            device_id_type=MESH,
        )

    @pl.loop(1, curves)
    def _(k):
        mean_copy(k).start()

    mall[cg] = msend[...]

    mean_row = jnp.concatenate(own_mean, axis=1)
    centred = coef_ref[...] - mean_row
    local[...] = centred
    stacked = jnp.concatenate([centred, jnp.broadcast_to(mean_row, (LANES, width))], axis=0)
    contract_last = (((1,), (1,)), ((), ()))
    partial = lax.dot_general(
        tt_ref[...],
        stacked,
        contract_last,
        precision=lax.Precision.HIGHEST,
        preferred_element_type=jnp.float32,
    )
    lsend[...] = partial.reshape(blocks, share, rows + LANES)

    def scatter_copy(k):
        to = lax.rem(tb + k, blocks)
        return pltpu.make_async_remote_copy(
            src_ref=lsend.at[to],
            dst_ref=lparts.at[tb],
            send_sem=rs_send.at[k],
            recv_sem=rs_recv.at[k],
            device_id={"tm": to},
            device_id_type=MESH,
        )

    def gather_copy(k):
        return pltpu.make_async_remote_copy(
            src_ref=lfull.at[tb],
            dst_ref=lfull.at[tb],
            send_sem=ag_send.at[k],
            recv_sem=ag_recv.at[k],
            device_id={"tm": lax.rem(tb + k, blocks)},
            device_id_type=MESH,
        )

    def shift_copy(k):
        return pltpu.make_async_remote_copy(
            src_ref=usend,
            dst_ref=uparts.at[tb],
            send_sem=u_send.at[k],
            recv_sem=u_recv.at[k],
            device_id={"tm": lax.rem(tb + k, blocks)},
            device_id_type=MESH,
        )

    def sketch_copy(k):
        to = lax.rem(cg + k, curves)
        return pltpu.make_async_remote_copy(
            src_ref=spack.at[pl.ds(pl.multiple_of(to * owned, owned), owned), :],
            dst_ref=sparts.at[cg],
            send_sem=f_send.at[k],
            recv_sem=f_recv.at[k],
            device_id={"curve": to},
            device_id_type=MESH,
        )

    @pl.loop(1, blocks)
    def _(k):
        scatter_copy(k).start()

    lparts[tb] = lsend[tb]

    @pl.loop(1, blocks)
    def _(k):
        scatter_copy(k).wait()

    lfull[tb] = jnp.sum(lparts[...], axis=0)

    @pl.loop(1, blocks)
    def _(k):
        gather_copy(k).start()

    @pl.loop(1, curves)
    def _(k):
        mean_copy(k).wait()

    means = mall[...]
    rough = jnp.sum(means, axis=0) / curves
    slip = jnp.sum(means - rough[None], axis=0) / curves
    apart = (msend[...] - rough) - slip
    apart_row = jnp.concatenate(
        [jnp.broadcast_to(apart[i : i + 1, :], (8, LANES)) for i in range(tiles)], axis=1
    )
    shift_part = lax.dot_general(
        apart_row,
        tt_ref[...],
        contract_last,
        precision=lax.Precision.HIGHEST,
        preferred_element_type=jnp.float32,
    )
    usend[...] = jnp.zeros_like(usend)
    usend[:, pl.ds(0, rank)] = shift_part

    @pl.loop(1, blocks)
    def _(k):
        shift_copy(k).start()

    uparts[tb] = usend[...]

    @pl.loop(1, blocks)
    def _(k):
        gather_copy(k).wait()

    full = lfull[...].reshape(rank, rows + LANES)
    inner_scores = full[:, :rows]
    group_scores = full[:, rows:]
    part = jnp.dot(
        inner_scores,
        local[...],
        precision=lax.Precision.HIGHEST,
        preferred_element_type=jnp.float32,
    )
    for i in range(tiles):
        between = group_scores * (float(rows) * apart[i : i + 1, :])
        spack[pl.ds(i, rank, stride=tiles), :] = part[:, i * LANES : (i + 1) * LANES] + between

    @pl.loop(1, curves)
    def _(k):
        sketch_copy(k).start()

    sparts[cg] = spack[pl.ds(pl.multiple_of(cg * owned, owned), owned), :]

    @pl.loop(1, blocks)
    def _(k):
        shift_copy(k).wait()

    shift = jnp.sum(uparts[...], axis=0)
    shift_col = jnp.transpose(jnp.broadcast_to(shift[0:1, :], (LANES, LANES)))[:rank, :1]
    score_ref[...] = inner_scores + shift_col

    @pl.loop(1, curves)
    def _(k):
        sketch_copy(k).wait()

    total = jnp.sum(sparts[...], axis=0) / (rows * curves)
    for p in range(rank // curves):
        for i in range(tiles):
            at = pl.ds(i * LANES, LANES)
            row = p * tiles + i
            sketch_ref[p : p + 1, at] = prev_ref[p : p + 1, at] + total[row : row + 1, :]


def body(curves, blocks, samples, smoothing, test_matrix, sketch_prev):
    rows, taken = samples.shape
    width = taken // SPB
    rank = test_matrix.shape[1]
    tiles = width // LANES
    chunks = taken // CHUNK
    group = rows // GROUPS
    share = rank // blocks
    owned = rank // curves * tiles
    line = min(rows, LANES)
    f32 = jnp.float32
    vmem = pl.BlockSpec(memory_space=pltpu.VMEM)
    anywhere = pl.BlockSpec(memory_space=pl.ANY)
    dma = pltpu.SemaphoreType.DMA
    coef, score_t, sketch_t = pl.pallas_call(
        functools.partial(kernel, curves, blocks),
        out_shape=(
            jax.ShapeDtypeStruct((rows, width), f32),
            jax.ShapeDtypeStruct((rank, rows), f32),
            jax.ShapeDtypeStruct((rank // curves, width), f32),
        ),
        in_specs=[anywhere, vmem, vmem, vmem, anywhere],
        out_specs=(vmem, vmem, vmem),
        scratch_shapes=[
            pltpu.VMEM((chunks, rows, CHUNK), f32),
            pltpu.VMEM((CHUNK, 2 * LANES), jnp.bfloat16),
            pltpu.VMEM((chunks, rows, LANES), f32),
            pltpu.VMEM((rows, LANES), f32),
            pltpu.VMEM((group, LANES), f32),
            pltpu.VMEM((group, LANES), f32),
            pltpu.VMEM((group, LANES), f32),
            pltpu.VMEM((group, LANES), f32),
            pltpu.VMEM((rows, width), f32),
            pltpu.VMEM((8, LANES), f32),
            pltpu.VMEM((curves, 8, LANES), f32),
            pltpu.VMEM((blocks, share, rows + LANES), f32),
            pltpu.VMEM((blocks, share, rows + LANES), f32),
            pltpu.VMEM((blocks, share, rows + LANES), f32),
            pltpu.VMEM((8, LANES), f32),
            pltpu.VMEM((blocks, 8, LANES), f32),
            pltpu.VMEM((rank * tiles, LANES), f32),
            pltpu.VMEM((curves, owned, LANES), f32),
            dma((chunks,)),
            dma,
            dma((2,)),
            dma((2,)),
            dma((curves,)),
            dma((curves,)),
            dma((blocks,)),
            dma((blocks,)),
            dma((blocks,)),
            dma((blocks,)),
            dma((blocks,)),
            dma((blocks,)),
            dma((curves,)),
            dma((curves,)),
        ],
        compiler_params=pltpu.CompilerParams(
            collective_id=0, has_side_effects=True, vmem_limit_bytes=48 * 1024 * 1024
        ),
    )(
        samples,
        smoothing.reshape(rows // line, line),
        test_matrix.T,
        sketch_prev.T,
        jnp.asarray(banded_table()),
    )
    return coef, score_t.T, sketch_t.T


def solution(mesh):
    placed = (P("curve", "tm"), P("curve"), P("tm", None), P("tm", "curve"))
    return jax.shard_map(
        functools.partial(body, mesh.shape["curve"], mesh.shape["tm"]),
        mesh=mesh,
        in_specs=placed,
        out_specs=(P("curve", "tm"), P("curve", None), P("tm", "curve")),
        check_vma=False,
    )
```

```python
import functools

import jax
import jax.numpy as jnp
import numpy as np
from jax import lax
from jax.experimental import pallas as pl
from jax.experimental.pallas import tpu as pltpu
from jax.sharding import PartitionSpec as P

SPB = 16
ITERS = 4
MARGIN = 2 * ITERS
LANES = 128
TILE = 8
CHUNK = 1024
SEGS = CHUNK // SPB
SPAN = SEGS + TILE
MESH = pl.DeviceIdType.MESH
CONTRACT_LAST = (((1,), (1,)), ((), ()))
damping = 0.45
TABLE_SCALE = 1.0 / (6.0 * 32.0**3 * SPB)


def banded_table():
    odd = 2 * np.arange(SPB, dtype=np.int64) + 1
    pieces = np.stack(
        [
            odd**3,
            -3 * odd**3 + 96 * odd**2 + 3072 * odd + 32768,
            3 * odd**3 - 192 * odd**2 + 4 * 32768,
            (32 - odd) ** 3,
        ]
    )
    band = np.zeros((SPAN, CHUNK), np.float64)
    for segment in range(SEGS):
        for m in range(4):
            band[segment + 3 - m, segment * SPB : (segment + 1) * SPB] = pieces[m]
    high = band.astype(jnp.bfloat16)
    low = (band - high.astype(np.float64)).astype(jnp.bfloat16)
    return np.concatenate([high, low], axis=0)


def split(value):
    high = value.astype(jnp.bfloat16)
    rest = value - high.astype(jnp.float32)
    middle = rest.astype(jnp.bfloat16)
    low = (rest - middle.astype(jnp.float32)).astype(jnp.bfloat16)
    return high, middle, low


def stacked_dot(parts, count, other, transposed):
    total = None
    for used, right in zip((3, 2, 1), other):
        left = parts[: used * count]
        if transposed:
            out = lax.dot_general(left, right, CONTRACT_LAST, preferred_element_type=jnp.float32)
        else:
            out = jnp.dot(left, right, preferred_element_type=jnp.float32)
        for i in range(used):
            piece = out[i * count : (i + 1) * count]
            total = piece if total is None else total + piece
    return total


def kernel(
    curves,
    blocks,
    x_hbm,
    s_hbm,
    tt_hbm,
    prev_hbm,
    w_hbm,
    coef_ref,
    score_ref,
    sketch_ref,
    xbuf,
    wbuf,
    sbuf,
    ttbuf,
    prevbuf,
    obuf,
    from_left,
    from_right,
    target,
    even,
    uneven,
    parts,
    msend,
    mall,
    lsend,
    lparts,
    lfull,
    usend,
    uparts,
    spack,
    sparts,
    x_sem,
    in_sem,
    halo_send,
    halo_recv,
    m_send,
    m_recv,
    rs_send,
    rs_recv,
    ag_send,
    ag_recv,
    u_send,
    u_recv,
    f_send,
    f_recv,
):
    rows, width = coef_ref.shape
    halves = rows // LANES
    tiles = width // LANES
    chunks = x_hbm.shape[1] // CHUNK
    rank = tt_hbm.shape[0]
    share = rank // blocks
    owned = rank // curves * tiles
    cg, tb = lax.axis_index("curve"), lax.axis_index("tm")
    left, right = lax.rem(tb + blocks - 1, blocks), lax.rem(tb + 1, blocks)

    def fetch(c):
        return pltpu.make_async_copy(x_hbm.at[:, pl.ds(c * CHUNK, CHUNK)], xbuf.at[c], x_sem.at[c])

    table_copy = pltpu.make_async_copy(w_hbm, wbuf, in_sem.at[0])
    small = [
        pltpu.make_async_copy(s_hbm, sbuf, in_sem.at[1]),
        pltpu.make_async_copy(tt_hbm, ttbuf, in_sem.at[2]),
        pltpu.make_async_copy(prev_hbm, prevbuf, in_sem.at[3]),
    ]
    table_copy.start()
    fetch(0).start()
    fetch(chunks - 1).start()
    for c in range(1, chunks - 1):
        fetch(c).start()
    for copy in small:
        copy.start()

    barrier = pltpu.get_barrier_semaphore()

    @pl.loop(1, blocks)
    def _(k):
        pl.semaphore_signal(
            barrier, inc=1, device_id={"tm": lax.rem(tb + k, blocks)}, device_id_type=MESH
        )

    @pl.loop(1, curves)
    def _(k):
        pl.semaphore_signal(
            barrier, inc=1, device_id={"curve": lax.rem(cg + k, curves)}, device_id_type=MESH
        )

    def project(c):
        fetch(c).wait()
        w = wbuf[...]
        total = None
        for part in split(xbuf[c]):
            out = lax.dot_general(w, part, CONTRACT_LAST, preferred_element_type=jnp.float32)
            total = out if total is None else total + out
        total = (total[:SPAN] + total[SPAN:]) * TABLE_SCALE
        for h in range(halves):
            obuf[c, h] = total[:, h * LANES : (h + 1) * LANES]

    table_copy.wait()
    project(0)
    project(chunks - 1)

    pl.semaphore_wait(barrier, blocks + curves - 2)

    def halo(side, source, to, device):
        return pltpu.make_async_remote_copy(
            src_ref=source,
            dst_ref=to,
            send_sem=halo_send.at[side],
            recv_sem=halo_recv.at[side],
            device_id={"tm": device},
            device_id_type=MESH,
        )

    edge_low = obuf.at[0, :, pl.ds(0, MARGIN), :]
    edge_high = obuf.at[chunks - 1, :, pl.ds(SEGS - MARGIN, 2 * MARGIN), :]
    send_left = halo(0, edge_low, from_right, left)
    send_right = halo(1, edge_high, from_left, right)
    send_left.start()
    send_right.start()

    @pl.loop(1, chunks - 1)
    def _(c):
        project(c)

    for copy in small:
        copy.wait()
    first, final = tb == 0, tb == blocks - 1
    row = lax.broadcasted_iota(jnp.int32, (TILE, LANES), 0)
    own = 2 * TILE
    size = width + 4 * TILE
    blank = jnp.zeros((TILE, LANES), jnp.float32)

    for buffer in (target, even, uneven):
        for h in range(halves):
            buffer[h, pl.ds(0, TILE), :] = blank
            buffer[h, pl.ds(size - TILE, TILE), :] = blank

    def put(h, at, value):
        target[h, at, :] = value
        even[h, at, :] = value

    for h in range(halves):
        for c in range(1, chunks):
            start = own + c * SEGS
            put(h, pl.ds(start, TILE), obuf[c, h, 0:TILE, :] + obuf[c - 1, h, SEGS:SPAN, :])
            put(h, pl.ds(start + TILE, SEGS - TILE), obuf[c, h, TILE:SEGS, :])
        put(h, pl.ds(own + TILE, SEGS - TILE), obuf[0, h, TILE:SEGS, :])

    send_left.wait()
    send_right.wait()
    for h in range(halves):
        halo_low = jnp.where(first, 0.0, from_left[h, 0:MARGIN, :])
        spilled = jnp.where(first, 0.0, from_left[h, MARGIN : 2 * MARGIN, :])
        halo_high = jnp.where(final, 0.0, from_right[h])
        put(h, pl.ds(own - TILE, TILE), halo_low)
        put(h, pl.ds(own, TILE), obuf[0, h, 0:TILE, :] + spilled)
        put(h, pl.ds(own + width, TILE), halo_high + obuf[chunks - 1, h, SEGS:SPAN, :])

    low_0, low_1 = first & (row == 0), first & (row == 1)
    top_0, top_1 = final & (row == TILE - 1), final & (row == TILE - 2)

    def sweep(source, result):
        for h in range(halves):
            s = jnp.broadcast_to(sbuf[h : h + 1, :], (TILE, LANES))
            inner = damping / (1.0 + 6.0 * s)
            near = damping / (1.0 + 5.0 * s)
            edge = damping / (1.0 + s)

            def moved(start, count, by):
                return source[h, pl.ds(start + by, count), :]

            def outer(start, count, off, rate, weight):
                pull = target[h, pl.ds(start, count), :] - weight * off
                value = (1.0 - damping) * moved(start, count, 0) + rate * pull
                result[h, pl.ds(start, count), :] = value

            def plain(start, count):
                far = moved(start, count, -2) + moved(start, count, 2)
                near_by = moved(start, count, -1) + moved(start, count, 1)
                grow = count // TILE
                rate = jnp.concatenate([inner] * grow, axis=0) if grow > 1 else inner
                weight = jnp.concatenate([s] * grow, axis=0) if grow > 1 else s
                outer(start, count, far - 4.0 * near_by, rate, weight)

            start = own
            below_2 = jnp.where(low_0 | low_1, 0.0, moved(start, TILE, -2))
            below_1 = jnp.where(low_0, 0.0, jnp.where(low_1, 2.0, 4.0) * moved(start, TILE, -1))
            above_1 = jnp.where(low_0, 2.0, 4.0) * moved(start, TILE, 1)
            off = below_2 + moved(start, TILE, 2) - (below_1 + above_1)
            outer(start, TILE, off, jnp.where(low_0, edge, jnp.where(low_1, near, inner)), s)
            start = own + width - TILE
            above_2 = jnp.where(top_0 | top_1, 0.0, moved(start, TILE, 2))
            above_1 = jnp.where(top_0, 0.0, jnp.where(top_1, 2.0, 4.0) * moved(start, TILE, 1))
            below_1 = jnp.where(top_0, 2.0, 4.0) * moved(start, TILE, -1)
            off = above_2 + moved(start, TILE, -2) - (below_1 + above_1)
            outer(start, TILE, off, jnp.where(top_0, edge, jnp.where(top_1, near, inner)), s)

            plain(own - TILE, TILE)
            plain(own + width, TILE)
            for start in range(own + TILE, own + width - TILE, TILE):
                plain(start, TILE)

    sweep(even, uneven)
    sweep(uneven, even)
    sweep(even, uneven)
    sweep(uneven, even)

    for h in range(halves):
        at = pl.ds(h * LANES, LANES)
        for i, part in enumerate(split(even[h, pl.ds(own, width), :])):
            parts[i, :, at] = part
    tt = ttbuf[...]
    tt_parts = jnp.concatenate(split(tt), axis=0)
    partial = stacked_dot(tt_parts, rank, [parts[i] for i in range(3)], False)
    lsend[...] = partial.reshape(blocks, share, rows)

    def scatter_copy(k):
        to = lax.rem(tb + k, blocks)
        return pltpu.make_async_remote_copy(
            src_ref=lsend.at[to],
            dst_ref=lparts.at[tb],
            send_sem=rs_send.at[k],
            recv_sem=rs_recv.at[k],
            device_id={"tm": to},
            device_id_type=MESH,
        )

    def gather_copy(k):
        return pltpu.make_async_remote_copy(
            src_ref=lfull.at[tb],
            dst_ref=lfull.at[tb],
            send_sem=ag_send.at[k],
            recv_sem=ag_recv.at[k],
            device_id={"tm": lax.rem(tb + k, blocks)},
            device_id_type=MESH,
        )

    def shift_copy(k):
        return pltpu.make_async_remote_copy(
            src_ref=usend,
            dst_ref=uparts.at[tb],
            send_sem=u_send.at[k],
            recv_sem=u_recv.at[k],
            device_id={"tm": lax.rem(tb + k, blocks)},
            device_id_type=MESH,
        )

    def mean_copy(k):
        return pltpu.make_async_remote_copy(
            src_ref=msend,
            dst_ref=mall.at[cg],
            send_sem=m_send.at[k],
            recv_sem=m_recv.at[k],
            device_id={"curve": lax.rem(cg + k, curves)},
            device_id_type=MESH,
        )

    def sketch_copy(k):
        to = lax.rem(cg + k, curves)
        return pltpu.make_async_remote_copy(
            src_ref=spack.at[pl.ds(pl.multiple_of(to * owned, owned), owned), :],
            dst_ref=sparts.at[cg],
            send_sem=f_send.at[k],
            recv_sem=f_recv.at[k],
            device_id={"curve": to},
            device_id_type=MESH,
        )

    @pl.loop(1, blocks)
    def _(k):
        scatter_copy(k).start()

    lparts[tb] = lsend[tb]

    lane = lax.broadcasted_iota(jnp.int32, (LANES, LANES), 1)
    line = lax.broadcasted_iota(jnp.int32, (LANES, LANES), 0)
    msend[...] = jnp.zeros_like(msend)
    for i in range(tiles):
        at = pl.ds(own + i * LANES, LANES)
        block = even[0, at, :]
        for h in range(1, halves):
            block += even[h, at, :]
        mean = jnp.sum(block, axis=1, keepdims=True) / rows
        msend[i : i + 1, :] = jnp.sum(jnp.where(lane == line, mean, 0.0), axis=0, keepdims=True)

    @pl.loop(1, curves)
    def _(k):
        mean_copy(k).start()

    mall[cg] = msend[...]

    for h in range(halves):
        for i in range(tiles):
            block = even[h, pl.ds(own + i * LANES, LANES), :]
            coef_ref[pl.ds(h * LANES, LANES), pl.ds(i * LANES, LANES)] = jnp.transpose(block)

    @pl.loop(1, blocks)
    def _(k):
        scatter_copy(k).wait()

    mine = jnp.sum(lparts[...], axis=0)
    group_score = jnp.sum(mine, axis=1, keepdims=True) / rows
    mine = mine - group_score
    slip = jnp.sum(mine, axis=1, keepdims=True) / rows
    lfull[tb] = jnp.concatenate(
        [mine - slip, jnp.broadcast_to(group_score + slip, (share, LANES))], axis=1
    )

    @pl.loop(1, blocks)
    def _(k):
        gather_copy(k).start()

    @pl.loop(1, curves)
    def _(k):
        mean_copy(k).wait()

    means = mall[...]
    rough = jnp.sum(means, axis=0) / curves
    slip = jnp.sum(means - rough[None], axis=0) / curves
    apart = (msend[...] - rough) - slip
    apart_row = jnp.concatenate(
        [jnp.broadcast_to(apart[i : i + 1, :], (TILE, LANES)) for i in range(tiles)], axis=1
    )
    shift_part = lax.dot_general(
        apart_row,
        tt,
        CONTRACT_LAST,
        precision=lax.Precision.HIGHEST,
        preferred_element_type=jnp.float32,
    )
    usend[...] = jnp.zeros_like(usend)
    usend[:, pl.ds(0, rank)] = shift_part

    @pl.loop(1, blocks)
    def _(k):
        shift_copy(k).start()

    uparts[tb] = usend[...]

    @pl.loop(1, blocks)
    def _(k):
        gather_copy(k).wait()

    full = lfull[...].reshape(rank, rows + LANES)
    inner_scores = full[:, :rows]
    group_scores = full[:, rows:]
    score_parts = jnp.concatenate(split(inner_scores), axis=0)
    part = stacked_dot(score_parts, rank, [parts[i] for i in range(3)], True)
    for i in range(tiles):
        between = group_scores * (float(rows) * apart[i : i + 1, :])
        spack[pl.ds(i, rank, stride=tiles), :] = part[:, i * LANES : (i + 1) * LANES] + between

    @pl.loop(1, curves)
    def _(k):
        sketch_copy(k).start()

    sparts[cg] = spack[pl.ds(pl.multiple_of(cg * owned, owned), owned), :]

    @pl.loop(1, blocks)
    def _(k):
        shift_copy(k).wait()

    shift = jnp.sum(uparts[...], axis=0)
    shift_col = jnp.transpose(jnp.broadcast_to(shift[0:1, :], (LANES, LANES)))[:rank, :1]
    score_ref[...] = inner_scores + shift_col

    @pl.loop(1, curves)
    def _(k):
        sketch_copy(k).wait()

    total = jnp.sum(sparts[...], axis=0) / (rows * curves)
    for p in range(rank // curves):
        for i in range(tiles):
            at = pl.ds(i * LANES, LANES)
            source = p * tiles + i
            sketch_ref[p : p + 1, at] = prevbuf[p : p + 1, at] + total[source : source + 1, :]


def finish(*refs):
    sources, results, sems = refs[:3], refs[3:6], refs[6]
    copies = [
        pltpu.make_async_copy(source, result, sems.at[i])
        for i, (source, result) in enumerate(zip(sources, results))
    ]
    for copy in copies:
        copy.start()
    for copy in copies:
        copy.wait()


def body(curves, blocks, samples, smoothing, test_matrix, sketch_prev):
    rows, taken = samples.shape
    width = taken // SPB
    rank = test_matrix.shape[1]
    halves = rows // LANES
    tiles = width // LANES
    chunks = taken // CHUNK
    share = rank // blocks
    owned = rank // curves * tiles
    f32 = jnp.float32
    vmem = pl.BlockSpec(memory_space=pltpu.VMEM)
    hbm = pl.BlockSpec(memory_space=pltpu.HBM)
    dma = pltpu.SemaphoreType.DMA
    tall = pltpu.VMEM((halves, width + 4 * TILE, LANES), f32)
    coef, score_t, sketch_t = pl.pallas_call(
        functools.partial(kernel, curves, blocks),
        out_shape=(
            jax.ShapeDtypeStruct((rows, width), f32),
            jax.ShapeDtypeStruct((rank, rows), f32),
            jax.ShapeDtypeStruct((rank // curves, width), f32),
        ),
        in_specs=[hbm] * 5,
        out_specs=(vmem, vmem, vmem),
        scratch_shapes=[
            pltpu.VMEM((chunks, rows, CHUNK), f32),
            pltpu.VMEM((2 * SPAN, CHUNK), jnp.bfloat16),
            pltpu.VMEM((halves, LANES), f32),
            pltpu.VMEM((rank, width), f32),
            pltpu.VMEM((rank // curves, width), f32),
            pltpu.VMEM((chunks, halves, SPAN, LANES), f32),
            pltpu.VMEM((halves, 2 * MARGIN, LANES), f32),
            pltpu.VMEM((halves, MARGIN, LANES), f32),
            tall,
            tall,
            tall,
            pltpu.VMEM((3, width, rows), jnp.bfloat16),
            pltpu.VMEM((TILE, LANES), f32),
            pltpu.VMEM((curves, TILE, LANES), f32),
            pltpu.VMEM((blocks, share, rows), f32),
            pltpu.VMEM((blocks, share, rows), f32),
            pltpu.VMEM((blocks, share, rows + LANES), f32),
            pltpu.VMEM((TILE, LANES), f32),
            pltpu.VMEM((blocks, TILE, LANES), f32),
            pltpu.VMEM((rank * tiles, LANES), f32),
            pltpu.VMEM((curves, owned, LANES), f32),
            dma((chunks,)),
            dma((4,)),
            dma((2,)),
            dma((2,)),
            dma((curves,)),
            dma((curves,)),
            dma((blocks,)),
            dma((blocks,)),
            dma((blocks,)),
            dma((blocks,)),
            dma((blocks,)),
            dma((blocks,)),
            dma((curves,)),
            dma((curves,)),
        ],
        compiler_params=pltpu.CompilerParams(
            collective_id=0, has_side_effects=True, vmem_limit_bytes=48 * 1024 * 1024
        ),
    )(
        *(
            pltpu.with_memory_space_constraint(value, pltpu.HBM)
            for value in (
                samples,
                smoothing.reshape(halves, LANES),
                test_matrix.T,
                sketch_prev.T,
                jnp.asarray(banded_table()),
            )
        )
    )
    coef, score_t, sketch_t = pl.pallas_call(
        finish,
        out_shape=(
            jax.ShapeDtypeStruct((rows, width), f32),
            jax.ShapeDtypeStruct((rank, rows), f32),
            jax.ShapeDtypeStruct((rank // curves, width), f32),
        ),
        in_specs=[vmem] * 3,
        out_specs=[hbm] * 3,
        scratch_shapes=[dma((3,))],
        compiler_params=pltpu.CompilerParams(vmem_limit_bytes=1048576),
    )(coef, score_t, sketch_t)
    return coef, score_t.T, sketch_t.T


def solution(mesh):
    placed = (P("curve", "tm"), P("curve"), P("tm", None), P("tm", "curve"))
    return jax.shard_map(
        functools.partial(body, mesh.shape["curve"], mesh.shape["tm"]),
        mesh=mesh,
        in_specs=placed,
        out_specs=(P("curve", "tm"), P("curve", None), P("tm", "curve")),
        check_vma=False,
    )
```

```python
import functools

import jax
import jax.numpy as jnp
import numpy as np
from jax import lax
from jax.experimental import pallas as pl
from jax.experimental.pallas import tpu as pltpu
from jax.sharding import PartitionSpec as P

SPB = 16
ITERS = 4
MARGIN = 2 * ITERS
LANES = 128
TILE = 8
CHUNK = 1024
SEGS = CHUNK // SPB
SPAN = SEGS + TILE
MESH = pl.DeviceIdType.MESH
CONTRACT_LAST = (((1,), (1,)), ((), ()))
damping = 0.45
TABLE_SCALE = 1.0 / (6.0 * 32.0**3 * SPB)


def banded_table():
    odd = 2 * np.arange(SPB, dtype=np.int64) + 1
    pieces = np.stack(
        [
            odd**3,
            -3 * odd**3 + 96 * odd**2 + 3072 * odd + 32768,
            3 * odd**3 - 192 * odd**2 + 4 * 32768,
            (32 - odd) ** 3,
        ]
    )
    band = np.zeros((SPAN, CHUNK), np.float64)
    for segment in range(SEGS):
        for m in range(4):
            band[segment + 3 - m, segment * SPB : (segment + 1) * SPB] = pieces[m]
    high = band.astype(jnp.bfloat16)
    low = (band - high.astype(np.float64)).astype(jnp.bfloat16)
    return np.concatenate([high, low], axis=0)


def split(value):
    high = value.astype(jnp.bfloat16)
    rest = value - high.astype(jnp.float32)
    middle = rest.astype(jnp.bfloat16)
    low = (rest - middle.astype(jnp.float32)).astype(jnp.bfloat16)
    return high, middle, low


def stacked_dot(parts, count, other, transposed):
    total = None
    for used, right in zip((3, 2, 1), other):
        left = parts[: used * count]
        if transposed:
            out = lax.dot_general(left, right, CONTRACT_LAST, preferred_element_type=jnp.float32)
        else:
            out = jnp.dot(left, right, preferred_element_type=jnp.float32)
        for i in range(used):
            piece = out[i * count : (i + 1) * count]
            total = piece if total is None else total + piece
    return total


def far_first(curves, act):
    quarter = curves // 4
    act(3 * quarter)
    act(quarter)

    @pl.loop(1, quarter)
    def _(d):
        act(3 * quarter + d)
        act(3 * quarter - d)
        act(quarter + d)
        act(quarter - d)

    act(2 * quarter)


def kernel(
    curves,
    blocks,
    x_hbm,
    s_hbm,
    tt_hbm,
    prev_hbm,
    w_hbm,
    coef_ref,
    score_ref,
    sketch_ref,
    xbuf,
    wbuf,
    sbuf,
    ttbuf,
    prevbuf,
    obuf,
    from_left,
    from_right,
    target,
    even,
    uneven,
    parts,
    msend,
    mall,
    lsend,
    lparts,
    lfull,
    usend,
    uparts,
    spack,
    sparts,
    x_sem,
    in_sem,
    halo_send,
    halo_recv,
    m_send,
    m_recv,
    rs_send,
    rs_recv,
    ag_send,
    ag_recv,
    u_send,
    u_recv,
    f_send,
    f_recv,
):
    rows, width = coef_ref.shape
    halves = rows // LANES
    tiles = width // LANES
    chunks = x_hbm.shape[1] // CHUNK
    rank = tt_hbm.shape[0]
    share = rank // blocks
    owned = rank // curves * tiles
    cg, tb = lax.axis_index("curve"), lax.axis_index("tm")
    left, right = lax.rem(tb + blocks - 1, blocks), lax.rem(tb + 1, blocks)

    def fetch(c):
        return pltpu.make_async_copy(x_hbm.at[:, pl.ds(c * CHUNK, CHUNK)], xbuf.at[c], x_sem.at[c])

    table_copy = pltpu.make_async_copy(w_hbm, wbuf, in_sem.at[0])
    small = [
        pltpu.make_async_copy(s_hbm, sbuf, in_sem.at[1]),
        pltpu.make_async_copy(tt_hbm, ttbuf, in_sem.at[2]),
        pltpu.make_async_copy(prev_hbm, prevbuf, in_sem.at[3]),
    ]
    table_copy.start()
    fetch(0).start()
    fetch(chunks - 1).start()
    for c in range(1, chunks - 1):
        fetch(c).start()
    for copy in small:
        copy.start()

    barrier = pltpu.get_barrier_semaphore()

    def greet(k):
        pl.semaphore_signal(
            barrier, inc=1, device_id={"curve": lax.rem(cg + k, curves)}, device_id_type=MESH
        )

    far_first(curves, greet)

    @pl.loop(1, blocks)
    def _(k):
        pl.semaphore_signal(
            barrier, inc=1, device_id={"tm": lax.rem(tb + k, blocks)}, device_id_type=MESH
        )

    def project(c):
        fetch(c).wait()
        w = wbuf[...]
        total = None
        for part in split(xbuf[c]):
            out = lax.dot_general(w, part, CONTRACT_LAST, preferred_element_type=jnp.float32)
            total = out if total is None else total + out
        total = (total[:SPAN] + total[SPAN:]) * TABLE_SCALE
        for h in range(halves):
            obuf[c, h] = total[:, h * LANES : (h + 1) * LANES]

    table_copy.wait()
    project(0)
    project(chunks - 1)

    pl.semaphore_wait(barrier, blocks + curves - 2)

    def halo(side, source, to, device):
        return pltpu.make_async_remote_copy(
            src_ref=source,
            dst_ref=to,
            send_sem=halo_send.at[side],
            recv_sem=halo_recv.at[side],
            device_id={"tm": device},
            device_id_type=MESH,
        )

    edge_low = obuf.at[0, :, pl.ds(0, MARGIN), :]
    edge_high = obuf.at[chunks - 1, :, pl.ds(SEGS - MARGIN, 2 * MARGIN), :]
    send_left = halo(0, edge_low, from_right, left)
    send_right = halo(1, edge_high, from_left, right)
    send_left.start()
    send_right.start()

    @pl.loop(1, chunks - 1)
    def _(c):
        project(c)

    for copy in small:
        copy.wait()
    first, final = tb == 0, tb == blocks - 1
    row = lax.broadcasted_iota(jnp.int32, (TILE, LANES), 0)
    own = 2 * TILE
    size = width + 4 * TILE
    blank = jnp.zeros((TILE, LANES), jnp.float32)

    for buffer in (target, even, uneven):
        for h in range(halves):
            buffer[h, pl.ds(0, TILE), :] = blank
            buffer[h, pl.ds(size - TILE, TILE), :] = blank

    def put(h, at, value):
        target[h, at, :] = value
        even[h, at, :] = value

    for h in range(halves):
        for c in range(1, chunks):
            start = own + c * SEGS
            put(h, pl.ds(start, TILE), obuf[c, h, 0:TILE, :] + obuf[c - 1, h, SEGS:SPAN, :])
            put(h, pl.ds(start + TILE, SEGS - TILE), obuf[c, h, TILE:SEGS, :])
        put(h, pl.ds(own + TILE, SEGS - TILE), obuf[0, h, TILE:SEGS, :])

    send_left.wait()
    send_right.wait()
    for h in range(halves):
        halo_low = jnp.where(first, 0.0, from_left[h, 0:MARGIN, :])
        spilled = jnp.where(first, 0.0, from_left[h, MARGIN : 2 * MARGIN, :])
        halo_high = jnp.where(final, 0.0, from_right[h])
        put(h, pl.ds(own - TILE, TILE), halo_low)
        put(h, pl.ds(own, TILE), obuf[0, h, 0:TILE, :] + spilled)
        put(h, pl.ds(own + width, TILE), halo_high + obuf[chunks - 1, h, SEGS:SPAN, :])

    low_0, low_1 = first & (row == 0), first & (row == 1)
    top_0, top_1 = final & (row == TILE - 1), final & (row == TILE - 2)

    def sweep(source, result):
        for h in range(halves):
            s = jnp.broadcast_to(sbuf[h : h + 1, :], (TILE, LANES))
            inner = damping / (1.0 + 6.0 * s)
            near = damping / (1.0 + 5.0 * s)
            edge = damping / (1.0 + s)

            def moved(start, count, by):
                return source[h, pl.ds(start + by, count), :]

            def outer(start, count, off, rate, weight):
                pull = target[h, pl.ds(start, count), :] - weight * off
                value = (1.0 - damping) * moved(start, count, 0) + rate * pull
                result[h, pl.ds(start, count), :] = value

            def plain(start, count):
                far = moved(start, count, -2) + moved(start, count, 2)
                near_by = moved(start, count, -1) + moved(start, count, 1)
                grow = count // TILE
                rate = jnp.concatenate([inner] * grow, axis=0) if grow > 1 else inner
                weight = jnp.concatenate([s] * grow, axis=0) if grow > 1 else s
                outer(start, count, far - 4.0 * near_by, rate, weight)

            start = own
            below_2 = jnp.where(low_0 | low_1, 0.0, moved(start, TILE, -2))
            below_1 = jnp.where(low_0, 0.0, jnp.where(low_1, 2.0, 4.0) * moved(start, TILE, -1))
            above_1 = jnp.where(low_0, 2.0, 4.0) * moved(start, TILE, 1)
            off = below_2 + moved(start, TILE, 2) - (below_1 + above_1)
            outer(start, TILE, off, jnp.where(low_0, edge, jnp.where(low_1, near, inner)), s)
            start = own + width - TILE
            above_2 = jnp.where(top_0 | top_1, 0.0, moved(start, TILE, 2))
            above_1 = jnp.where(top_0, 0.0, jnp.where(top_1, 2.0, 4.0) * moved(start, TILE, 1))
            below_1 = jnp.where(top_0, 2.0, 4.0) * moved(start, TILE, -1)
            off = above_2 + moved(start, TILE, -2) - (below_1 + above_1)
            outer(start, TILE, off, jnp.where(top_0, edge, jnp.where(top_1, near, inner)), s)

            plain(own - TILE, TILE)
            plain(own + width, TILE)
            for start in range(own + TILE, own + width - TILE, TILE):
                plain(start, TILE)

    sweep(even, uneven)
    sweep(uneven, even)
    sweep(even, uneven)
    sweep(uneven, even)

    for h in range(halves):
        at = pl.ds(h * LANES, LANES)
        for i, part in enumerate(split(even[h, pl.ds(own, width), :])):
            parts[i, :, at] = part
    lane = lax.broadcasted_iota(jnp.int32, (LANES, LANES), 1)
    line = lax.broadcasted_iota(jnp.int32, (LANES, LANES), 0)
    for i in range(tiles):
        at = pl.ds(own + i * LANES, LANES)
        block = even[0, at, :]
        for h in range(1, halves):
            block += even[h, at, :]
        mean = jnp.sum(block, axis=1, keepdims=True) / rows
        msend[i : i + 1, :] = jnp.sum(jnp.where(lane == line, mean, 0.0), axis=0, keepdims=True)

    tt = ttbuf[...]
    tt_parts = jnp.concatenate(split(tt), axis=0)
    partial = stacked_dot(tt_parts, rank, [parts[i] for i in range(3)], False)
    lsend[...] = partial.reshape(blocks, share, rows)

    def scatter_copy(k):
        to = lax.rem(tb + k, blocks)
        return pltpu.make_async_remote_copy(
            src_ref=lsend.at[to],
            dst_ref=lparts.at[tb],
            send_sem=rs_send.at[k],
            recv_sem=rs_recv.at[k],
            device_id={"tm": to},
            device_id_type=MESH,
        )

    def gather_copy(k):
        return pltpu.make_async_remote_copy(
            src_ref=lfull.at[tb],
            dst_ref=lfull.at[tb],
            send_sem=ag_send.at[k],
            recv_sem=ag_recv.at[k],
            device_id={"tm": lax.rem(tb + k, blocks)},
            device_id_type=MESH,
        )

    def shift_copy(k):
        return pltpu.make_async_remote_copy(
            src_ref=usend,
            dst_ref=uparts.at[tb],
            send_sem=u_send.at[k],
            recv_sem=u_recv.at[k],
            device_id={"tm": lax.rem(tb + k, blocks)},
            device_id_type=MESH,
        )

    def mean_copy(k):
        return pltpu.make_async_remote_copy(
            src_ref=msend,
            dst_ref=mall.at[cg],
            send_sem=m_send.at[k],
            recv_sem=m_recv.at[k],
            device_id={"curve": lax.rem(cg + k, curves)},
            device_id_type=MESH,
        )

    def sketch_copy(source, to):
        return pltpu.make_async_remote_copy(
            src_ref=spack.at[pl.ds(pl.multiple_of(to * owned, owned), owned), :],
            dst_ref=sparts.at[source],
            send_sem=f_send.at[to],
            recv_sem=f_recv.at[source],
            device_id={"curve": to},
            device_id_type=MESH,
        )

    def sketch_of(chunks_at, scores):
        count = len(chunks_at) * share
        stacked = jnp.concatenate([p.astype(jnp.float32) for p in split(scores)], axis=0)
        stacked = stacked.astype(jnp.bfloat16)
        total = None
        for used, i in ((3, 0), (2, 1), (1, 2)):
            out = lax.dot_general(
                stacked, parts[i], CONTRACT_LAST, preferred_element_type=jnp.float32
            )
            for n in range(used):
                piece = out[n * count : (n + 1) * count]
                total = piece if total is None else total + piece
        for n, chunk in enumerate(chunks_at):
            for i in range(tiles):
                at = pl.ds(chunk * (share * tiles) + i, share, stride=tiles)
                spack[at, :] = total[n * share : (n + 1) * share, i * LANES : (i + 1) * LANES]
        for chunk in chunks_at:
            for n in range(curves // blocks):
                to = chunk * (curves // blocks) + n

                @pl.when(to != cg)
                def _(to=to):
                    sketch_copy(cg, to).start()

    @pl.loop(1, blocks)
    def _(k):
        scatter_copy(k).start()

    far_first(curves, lambda k: mean_copy(k).start())
    lparts[tb] = lsend[tb]
    mall[cg] = msend[...]

    for h in range(halves):
        for i in range(tiles):
            block = even[h, pl.ds(own + i * LANES, LANES), :]
            coef_ref[pl.ds(h * LANES, LANES), pl.ds(i * LANES, LANES)] = jnp.transpose(block)

    @pl.loop(1, blocks)
    def _(k):
        scatter_copy(k).wait()

    mine = jnp.sum(lparts[...], axis=0)
    mine = mine - jnp.sum(mine, axis=1, keepdims=True) / rows
    mine = mine - jnp.sum(mine, axis=1, keepdims=True) / rows
    lfull[tb] = mine

    @pl.loop(1, blocks)
    def _(k):
        gather_copy(k).start()

    sketch_of([tb], mine)
    near_first = [[4, 1, 7], [3, 5], [2, 6]] if blocks == 8 else [list(range(1, blocks))]
    for distances in near_first:
        for k in distances:
            gather_copy(blocks - k).wait_recv()
        chunks_at = [lax.rem(tb + k, blocks) for k in distances]
        sketch_of(chunks_at, jnp.concatenate([lfull[c] for c in chunks_at], axis=0))
    sparts[cg] = spack[pl.ds(pl.multiple_of(cg * owned, owned), owned), :]

    @pl.loop(1, curves)
    def _(k):
        mean_copy(k).wait()

    apart = []
    for i in range(tiles):
        about = mall[:, i, :]
        about = about - jnp.sum(about, axis=0, keepdims=True) / curves
        apart.append(about - jnp.sum(about, axis=0, keepdims=True) / curves)
    exact = dict(precision=lax.Precision.HIGHEST, preferred_element_type=jnp.float32)
    shifts = lax.dot_general(jnp.concatenate(apart, axis=1), tt, CONTRACT_LAST, **exact)
    group_at = lax.broadcasted_iota(jnp.int32, (curves, rank), 0)
    per_owner = rank // curves
    picks = usend.shape[1]
    column = lax.broadcasted_iota(jnp.int32, (picks, rank), 1)
    pick = lax.broadcasted_iota(jnp.int32, (picks, rank), 0)
    chosen = (column == cg * per_owner + pick) & (pick < per_owner)
    usend[...] = jnp.zeros_like(usend)
    usend[0, :, pl.ds(0, rank)] = jnp.broadcast_to(
        jnp.sum(jnp.where(group_at == cg, shifts, 0.0), axis=0, keepdims=True), (picks, rank)
    )
    usend[1, :, pl.ds(0, curves)] = lax.dot_general(
        chosen.astype(jnp.float32), shifts, CONTRACT_LAST, **exact
    )

    @pl.loop(1, blocks)
    def _(k):
        shift_copy(k).start()

    uparts[tb] = usend[...]

    @pl.loop(1, blocks)
    def _(k):
        shift_copy(k).wait()
        gather_copy(k).wait_send()

    shift = jnp.sum(uparts[...], axis=0)
    shift_col = jnp.transpose(jnp.broadcast_to(shift[0, 0:1, :], (LANES, LANES)))[:rank, :1]
    score_ref[...] = lfull[...].reshape(rank, rows) + shift_col
    between = [
        jnp.dot(shift[1, :, :curves], apart[i], **exact) / curves for i in range(tiles)
    ]

    @pl.loop(1, curves)
    def _(k):
        other = lax.rem(cg + k, curves)
        sketch_copy(other, other).wait()

    total = jnp.sum(sparts[...], axis=0) / (rows * curves)
    for p in range(per_owner):
        for i in range(tiles):
            at = pl.ds(i * LANES, LANES)
            source = p * tiles + i
            summed = total[source : source + 1, :] + between[i][p : p + 1, :]
            sketch_ref[p : p + 1, at] = prevbuf[p : p + 1, at] + summed


def finish(*refs):
    sources, results, sems = refs[:3], refs[3:6], refs[6]
    copies = [
        pltpu.make_async_copy(source, result, sems.at[i])
        for i, (source, result) in enumerate(zip(sources, results))
    ]
    for copy in copies:
        copy.start()
    for copy in copies:
        copy.wait()


def body(curves, blocks, samples, smoothing, test_matrix, sketch_prev):
    rows, taken = samples.shape
    width = taken // SPB
    rank = test_matrix.shape[1]
    halves = rows // LANES
    tiles = width // LANES
    chunks = taken // CHUNK
    share = rank // blocks
    owned = rank // curves * tiles
    picks = -(-(rank // curves) // TILE) * TILE
    f32 = jnp.float32
    vmem = pl.BlockSpec(memory_space=pltpu.VMEM)
    hbm = pl.BlockSpec(memory_space=pltpu.HBM)
    dma = pltpu.SemaphoreType.DMA
    tall = pltpu.VMEM((halves, width + 4 * TILE, LANES), f32)
    coef, score_t, sketch_t = pl.pallas_call(
        functools.partial(kernel, curves, blocks),
        out_shape=(
            jax.ShapeDtypeStruct((rows, width), f32),
            jax.ShapeDtypeStruct((rank, rows), f32),
            jax.ShapeDtypeStruct((rank // curves, width), f32),
        ),
        in_specs=[hbm] * 5,
        out_specs=(vmem, vmem, vmem),
        scratch_shapes=[
            pltpu.VMEM((chunks, rows, CHUNK), f32),
            pltpu.VMEM((2 * SPAN, CHUNK), jnp.bfloat16),
            pltpu.VMEM((halves, LANES), f32),
            pltpu.VMEM((rank, width), f32),
            pltpu.VMEM((rank // curves, width), f32),
            pltpu.VMEM((chunks, halves, SPAN, LANES), f32),
            pltpu.VMEM((halves, 2 * MARGIN, LANES), f32),
            pltpu.VMEM((halves, MARGIN, LANES), f32),
            tall,
            tall,
            tall,
            pltpu.VMEM((3, width, rows), jnp.bfloat16),
            pltpu.VMEM((tiles, LANES), f32),
            pltpu.VMEM((curves, tiles, LANES), f32),
            pltpu.VMEM((blocks, share, rows), f32),
            pltpu.VMEM((blocks, share, rows), f32),
            pltpu.VMEM((blocks, share, rows), f32),
            pltpu.VMEM((2, picks, LANES), f32),
            pltpu.VMEM((blocks, 2, picks, LANES), f32),
            pltpu.VMEM((rank * tiles, LANES), f32),
            pltpu.VMEM((curves, owned, LANES), f32),
            dma((chunks,)),
            dma((4,)),
            dma((2,)),
            dma((2,)),
            dma((curves,)),
            dma((curves,)),
            dma((blocks,)),
            dma((blocks,)),
            dma((blocks,)),
            dma((blocks,)),
            dma((blocks,)),
            dma((blocks,)),
            dma((curves,)),
            dma((curves,)),
        ],
        compiler_params=pltpu.CompilerParams(
            collective_id=0, has_side_effects=True, vmem_limit_bytes=48 * 1024 * 1024
        ),
    )(
        *(
            pltpu.with_memory_space_constraint(value, pltpu.HBM)
            for value in (
                samples,
                smoothing.reshape(halves, LANES),
                test_matrix.T,
                sketch_prev.T,
                jnp.asarray(banded_table()),
            )
        )
    )
    coef, score_t, sketch_t = pl.pallas_call(
        finish,
        out_shape=(
            jax.ShapeDtypeStruct((rows, width), f32),
            jax.ShapeDtypeStruct((rank, rows), f32),
            jax.ShapeDtypeStruct((rank // curves, width), f32),
        ),
        in_specs=[vmem] * 3,
        out_specs=[hbm] * 3,
        scratch_shapes=[dma((3,))],
        compiler_params=pltpu.CompilerParams(vmem_limit_bytes=1048576),
    )(coef, score_t, sketch_t)
    return coef, score_t.T, sketch_t.T


def solution(mesh):
    placed = (P("curve", "tm"), P("curve"), P("tm", None), P("tm", "curve"))
    return jax.shard_map(
        functools.partial(body, mesh.shape["curve"], mesh.shape["tm"]),
        mesh=mesh,
        in_specs=placed,
        out_specs=(P("curve", "tm"), P("curve", None), P("tm", "curve")),
        check_vma=False,
    )
```
